32 devices in a mesh: dom: 16 (over z, y, x), feat: 2 (over core).
Axes of the slice: x: 2, y: 2, z: 4, core: 2. Of those that a mesh axis runs over, the one named last changes fastest.
Arguments:
- features: bfloat16 [16384, 512], P('dom', 'feat'), may hold values from -6 to 6
- grad_out: bfloat16 [16384, 512], P('dom', 'feat'), may hold values from -6 to 6
- pre_act: bfloat16 [16384, 512], P('dom', 'feat'), may hold values from -6 to 6
- neigh_mean: bfloat16 [16384, 512], P('dom', 'feat'), may hold values from -6 to 6
- w_self: bfloat16 [512, 512], P('feat'), may hold values from -0.25 to 0.25
- w_neigh: bfloat16 [512, 512], P('feat'), may hold values from -0.25 to 0.25
- edge_from: int32 [131072], P('dom'), may hold values from 0 to 1535
- edge_to: int32 [131072], P('dom'), may hold values from 0 to 1535
- edge_count: int32 [16], P('dom'), may hold values from 2048 to 8192, as said below
- mirror_master: int32 [8192], P('dom'), may hold values from 0 to 63
- degrees: int32 [16384], P('dom'), may hold values from 1 to 16
Outputs:
- input_grad: bfloat16 [16384, 512], P('dom', 'feat')
- self_weight_grad: float32 [512, 512], P('feat')
- neigh_weight_grad: float32 [512, 512], P('feat')
The draws below stay inside these ranges and needn't reach their ends.
Inputs may be any that keep to these rules, and one draw needn't show every extreme that they name: `edge_count`: equals 8192 in at least one partition.
All inputs are finite; a program needn't handle non-finite values.
Results may differ from the reference program's by a relative error of at most 0.0044.
Values may be sent and summed in bfloat16 or wider, within the bound.
A program may use at most 64 MiB of HBM per device.

```python
import math
import jax
import jax.numpy as jnp
import numpy as np
from jax import lax

D = 512
M_DEV = 1024
SLOT = 32
HUB = 64
E_DEV = 8192
LOCAL = 1536
NV = 16384
NE = 131072
N_DOM = 16


def draw_edge_count(key, part):
    counts = jax.random.randint(key, (N_DOM,), E_DEV // 4, E_DEV + 1)
    chosen = jax.random.randint(jax.random.fold_in(key, 7), (), 0, N_DOM)
    return counts.at[chosen].set(E_DEV).astype(jnp.int32)


def place_ends(drawn, key, smallest, top_value):
    spot = [jax.random.randint(jax.random.fold_in(key, axis), (), 0, length) for axis, length in enumerate(drawn.shape)]
    main_axis = drawn.shape.index(max(drawn.shape))
    beside = spot[:main_axis] + [(spot[main_axis] + 1) % drawn.shape[main_axis]] + spot[main_axis + 1:]
    return drawn.at[tuple(spot)].set(smallest).at[tuple(beside)].set(top_value)


def shard_levels(stream_key, extent, shards, smallest, largest):
    level = 1.0
    for axis_at, blocks in shards:
        draws = jax.random.uniform(jax.random.fold_in(jax.random.fold_in(stream_key, 6), axis_at), (blocks,), jnp.float32, smallest / len(shards), largest / len(shards))
        level = level * jnp.repeat(jnp.exp(draws), extent[axis_at] // blocks).reshape((-1,) + (1,) * (len(extent) - 1 - axis_at))
    return level


def rank_table(count, skew):
    loads = [(1 << 20) // math.isqrt(grade ** skew) + 1 for grade in range(1, count + 1)]
    deviation = 1 + sum(loads) // (1 << 30)
    return np.cumsum(np.array([max(1, weight // deviation) for weight in loads]))


def ranked(own_key, extent, amount, lean):
    table = rank_table(amount, lean)
    lot = jax.random.randint(jax.random.fold_in(own_key, 1), extent, 0, int(table[amount - 1]))
    standing = jnp.searchsorted(jnp.asarray(table, jnp.int32), lot, side="right")
    return jax.random.permutation(jax.random.fold_in(own_key, 2), amount)[standing].astype(jnp.int32)


def scatter_about(key, extent, deviation, limit, shards=(), kind=jnp.bfloat16):
    entries = deviation * jax.random.normal(key, extent, jnp.float32)
    if shards:
        entries = entries * shard_levels(key, extent, shards, -0.22, 0.18)
    return jnp.clip(entries, -limit, limit).astype(kind)


def setup_inputs(seed: int = 0) -> dict:
    keys = jax.random.split(jax.random.key(seed), 12)
    return {
        "features": scatter_about(keys[0], (NV, D), 1.0, 6.0, ((0, 16), (1, 2))),
        "grad_out": scatter_about(keys[1], (NV, D), 1.0, 6.0, ((0, 16), (1, 2))),
        "pre_act": scatter_about(keys[2], (NV, D), 1.0, 6.0, ((0, 16), (1, 2))),
        "neigh_mean": scatter_about(keys[3], (NV, D), 1.0, 6.0, ((0, 16), (1, 2))),
        "w_self": scatter_about(keys[4], (D, D), D ** -0.5, 0.25, ((0, 2),)),
        "w_neigh": scatter_about(keys[5], (D, D), D ** -0.5, 0.25, ((0, 2),)),
        "edge_from": place_ends(jax.random.randint(keys[6], (NE,), 0, LOCAL), jax.random.fold_in(keys[6], 1), 0, LOCAL - 1).astype(jnp.int32),
        "edge_to": place_ends(ranked(keys[7], (NE,), LOCAL, 2), jax.random.fold_in(keys[7], 3), 0, LOCAL - 1).astype(jnp.int32),
        "edge_count": draw_edge_count(jax.random.fold_in(keys[11], 71), 0),
        "mirror_master": place_ends(jax.random.randint(keys[9], (N_DOM * N_DOM * SLOT,), 0, HUB), jax.random.fold_in(keys[9], 1), 0, HUB - 1).astype(jnp.int32),
        "degrees": place_ends(jax.random.randint(keys[10], (NV,), 1, 17), jax.random.fold_in(keys[10], 1), 1, 16).astype(jnp.int32),
    }


def reference(features, grad_out, pre_act, neigh_mean, w_self, w_neigh, edge_from, edge_to, edge_count, mirror_master, degrees):
    grad_pre = (grad_out.astype(jnp.float32) * (pre_act > 0).astype(jnp.float32)).astype(jnp.bfloat16)
    self_weight_grad = jnp.dot(features.T, grad_pre, preferred_element_type=jnp.float32)
    neigh_weight_grad = jnp.dot(neigh_mean.T, grad_pre, preferred_element_type=jnp.float32)
    self_part = jnp.dot(grad_pre, w_self.T, preferred_element_type=jnp.float32)
    neigh_part = jnp.dot(grad_pre, w_neigh.T, preferred_element_type=jnp.float32)
    scaled = (neigh_part / degrees[:, None].astype(jnp.float32)).astype(jnp.bfloat16)
    mirror_count = N_DOM * SLOT
    local_rows = M_DEV + mirror_count
    owners = jnp.arange(mirror_count, dtype=jnp.int32) // SLOT

    def partition_step(index, totals):
        index = jnp.asarray(index).astype(jnp.int32)
        row_base = (index * M_DEV).astype(jnp.int32)
        masters = lax.dynamic_slice_in_dim(scaled, row_base, M_DEV, 0)
        targets = lax.dynamic_slice_in_dim(mirror_master, (index * mirror_count).astype(jnp.int32), mirror_count, 0)
        global_rows = (owners * M_DEV + targets).astype(jnp.int32)
        tables = jnp.concatenate([masters, scaled[global_rows]], axis=0)
        edge_base = (index * E_DEV).astype(jnp.int32)
        sources = lax.dynamic_slice_in_dim(edge_from, edge_base, E_DEV, 0)
        sinks = lax.dynamic_slice_in_dim(edge_to, edge_base, E_DEV, 0)
        is_live = jnp.arange(E_DEV, dtype=jnp.int32) < edge_count[index]
        contrib = jnp.where(is_live[:, None], tables[sinks].astype(jnp.float32), jnp.float32(0.0))
        summed = jax.ops.segment_sum(contrib, sources, num_segments=local_rows)
        mirror_grad = lax.optimization_barrier(summed[M_DEV:].astype(jnp.bfloat16)).astype(jnp.float32)
        current = lax.dynamic_slice_in_dim(totals, row_base, M_DEV, 0)
        totals = lax.dynamic_update_slice_in_dim(totals, current + summed[:M_DEV], row_base, 0)
        return totals.at[global_rows].add(mirror_grad)

    edge_grad = lax.fori_loop(0, N_DOM, partition_step, jnp.zeros((M_DEV * N_DOM, D), jnp.float32))
    input_grad = (self_part + edge_grad).astype(jnp.bfloat16)
    return input_grad, self_weight_grad, neigh_weight_grad
```

```python
import functools

import jax
import jax.numpy as jnp
from jax import lax
from jax.experimental import pallas as pl
from jax.experimental.pallas import tpu as pltpu
from jax.sharding import PartitionSpec as P


LANES = 128
HUBS = 64


def edge_kernel(block, limit_ref, table_ref, sink_ref, source_ref, out_ref):
    rows = table_ref.shape[0]
    groups = block // LANES
    one, zero = jnp.bfloat16(1.0), jnp.bfloat16(0.0)
    limit = limit_ref[0]
    out_ref[...] = jnp.zeros_like(out_ref)

    def step(b, carry):
        at = pl.ds(pl.multiple_of(b * groups, groups), groups)
        sinks, sources = sink_ref[at, :], source_ref[at, :]
        shape = (groups, LANES)
        place = (
            lax.broadcasted_iota(jnp.int32, shape, 0) * LANES
            + lax.broadcasted_iota(jnp.int32, shape, 1)
            + b * block
        )
        sources = jnp.where(place < limit, sources, -1)
        lane = lax.broadcasted_iota(jnp.int32, (LANES, LANES), 1)
        pick = []
        for g in range(groups):
            column = jnp.transpose(jnp.broadcast_to(sinks[g : g + 1, :], (LANES, LANES)))
            pick.append(
                jnp.concatenate(
                    [
                        jnp.where(column == lane + j, one, zero)
                        for j in range(0, rows, LANES)
                    ],
                    axis=1,
                )
            )
        pick = jnp.concatenate(pick, axis=0)
        gathered = jnp.dot(pick, table_ref[...], preferred_element_type=jnp.float32)
        row = lax.broadcasted_iota(jnp.int32, (rows, LANES), 0)
        put = jnp.concatenate(
            [jnp.where(row == sources[g : g + 1, :], one, zero) for g in range(groups)], axis=1
        )
        out_ref[...] += jnp.dot(
            put, gathered.astype(jnp.bfloat16), preferred_element_type=jnp.float32
        )
        return carry

    lax.fori_loop(0, sink_ref.shape[0] // groups, step, 0)


def edge_sums(limit, table, sinks, sources):
    edges = sinks.shape[0]
    vmem = pl.BlockSpec(memory_space=pltpu.VMEM)
    return pl.pallas_call(
        functools.partial(edge_kernel, 1024 if table.shape[0] <= 2048 else 256),
        out_shape=jax.ShapeDtypeStruct(table.shape, jnp.float32),
        in_specs=[pl.BlockSpec(memory_space=pltpu.SMEM), vmem, vmem, vmem],
        out_specs=vmem,
        compiler_params=pltpu.CompilerParams(vmem_limit_bytes=60 * 2**20),
    )(limit, table, sinks.reshape(-1, LANES), sources.reshape(-1, LANES))


def on_device(
    features,
    grad_out,
    pre_act,
    neigh_mean,
    w_self,
    w_neigh,
    edge_from,
    edge_to,
    edge_count,
    mirror_master,
    degrees,
):
    masters = features.shape[0]
    width_loc = features.shape[1]
    parts = lax.axis_size("dom")
    mirror_count = mirror_master.shape[0]
    slots = mirror_count // parts
    grad_pre = (grad_out.astype(jnp.float32) * (pre_act > 0).astype(jnp.float32)).astype(
        jnp.bfloat16
    )
    wanted = mirror_master.reshape(parts, slots)
    asked = lax.all_to_all(wanted, "dom", split_axis=0, concat_axis=0, tiled=True)
    block_cols = lax.all_gather(grad_pre, "feat", axis=1, tiled=True)
    contract = (((1,), (1,)), ((), ()))
    self_sum = lax.dot_general(block_cols, w_self, contract, preferred_element_type=jnp.float32)
    neigh_sum = lax.dot_general(block_cols, w_neigh, contract, preferred_element_type=jnp.float32)
    over_rows = (((0,), (0,)), ((), ()))
    grad_self = lax.dot_general(features, block_cols, over_rows, preferred_element_type=jnp.float32)
    grad_neigh = lax.dot_general(
        neigh_mean, block_cols, over_rows, preferred_element_type=jnp.float32
    )
    self_part, neigh_part, grad_self, grad_neigh = (self_sum, neigh_sum, grad_self, grad_neigh)
    scaled = (neigh_part / degrees[:, None].astype(jnp.float32)).astype(jnp.bfloat16)
    replies = scaled[asked.reshape(-1)].reshape(parts, slots, width_loc)
    mirror_rows = lax.all_to_all(replies, "dom", split_axis=0, concat_axis=0, tiled=True).reshape(
        mirror_count, width_loc
    )
    tables = jnp.concatenate([scaled, mirror_rows], axis=0)
    summed = edge_sums(edge_count, tables, edge_to, edge_from)
    mirror_grad = summed[masters:].astype(jnp.bfloat16)
    returned = lax.all_to_all(
        mirror_grad.reshape(parts, slots, width_loc), "dom", split_axis=0, concat_axis=0, tiled=True
    )
    hit = (jnp.arange(HUBS, dtype=jnp.int32)[:, None] == asked.reshape(1, -1)).astype(jnp.bfloat16)
    hub_add = jnp.dot(
        hit, returned.reshape(mirror_count, width_loc), preferred_element_type=jnp.float32
    )
    total = self_part + summed[:masters]
    input_grad = jnp.concatenate([total[:HUBS] + hub_add, total[HUBS:]], axis=0).astype(jnp.bfloat16)
    self_weight_grad, neigh_weight_grad = lax.psum((grad_self, grad_neigh), "dom")
    return (input_grad, self_weight_grad, neigh_weight_grad)


def solution(mesh):
    placed = (
        P("dom", "feat"),
        P("dom", "feat"),
        P("dom", "feat"),
        P("dom", "feat"),
        P("feat", None),
        P("feat", None),
        P("dom"),
        P("dom"),
        P("dom"),
        P("dom"),
        P("dom"),
    )
    return jax.shard_map(
        on_device,
        mesh=mesh,
        in_specs=placed,
        out_specs=(P("dom", "feat"), P("feat", None), P("feat", None)),
        check_vma=False,
    )
```

```python
import functools

import jax
import jax.numpy as jnp
from jax import lax
from jax.experimental import pallas as pl
from jax.experimental.pallas import tpu as pltpu
from jax.sharding import PartitionSpec as P

LANES = 128
HUBS = 64
MESH = pl.DeviceIdType.MESH
F32, BF16 = jnp.float32, jnp.bfloat16


def dot(a, b, over):
    return lax.dot_general(a, b, ((over[:1], over[1:]), ((), ())), preferred_element_type=F32)


def columns_of(row):
    return jnp.transpose(jnp.broadcast_to(row, (LANES, LANES)))


def pick_rows(sinks, first, count):
    one, zero = jnp.ones((), BF16), jnp.zeros((), BF16)
    lane = lax.broadcasted_iota(jnp.int32, (LANES, LANES), 1)
    tiles = []
    for g in range(sinks.shape[0]):
        column = columns_of(sinks[g : g + 1, :])
        tiles.append(
            jnp.concatenate(
                [jnp.where(column == lane + (first + j), one, zero) for j in range(0, count, LANES)],
                axis=1,
            )
        )
    return jnp.concatenate(tiles, axis=0)


def put_rows(sources, first, count):
    one, zero = jnp.ones((), BF16), jnp.zeros((), BF16)
    row = lax.broadcasted_iota(jnp.int32, (count, LANES), 0) + first
    return jnp.concatenate(
        [jnp.where(row == sources[g : g + 1, :], one, zero) for g in range(sources.shape[0])],
        axis=1,
    )


def layer_kernel(
    parts,
    block,
    limit_ref,
    grad_ref,
    pre_ref,
    features_ref,
    mean_ref,
    w_self_ref,
    w_neigh_ref,
    source_ref,
    sink_ref,
    wanted_ref,
    degree_ref,
    out_ref,
    weights_ref,
    cols,
    live,
    table,
    asked,
    replies,
    mirrors,
    picked,
    master_sum,
    mirror_sum,
    returns,
    returned,
    partial,
    arrived,
    summed,
    feat_sems,
    send_sems,
    recv_sems,
):
    me, half = lax.axis_index("dom"), lax.axis_index("feat")
    partner = 1 - half
    masters, width = grad_ref.shape
    slots = wanted_ref.shape[2]
    chunks, chunk = partial.shape[0], partial.shape[1]
    groups = block // LANES
    blocks = sink_ref.shape[0] // groups

    def peer(k):
        return lax.rem(me + k, parts)

    def giver(k):
        return lax.rem(me + (parts - k), parts)

    def rows_of(q):
        return pl.ds(pl.multiple_of(q * slots, slots), slots)

    def copy(stage, k, src, dst):
        return pltpu.make_async_remote_copy(
            src_ref=src,
            dst_ref=dst,
            send_sem=send_sems.at[stage, k],
            recv_sem=recv_sems.at[stage, k],
            device_id={"dom": peer(k)},
            device_id_type=MESH,
        )

    def each_peer(act):
        lax.fori_loop(1, parts, lambda k, c: (act(k), c)[1], 0)

    barrier = pltpu.get_barrier_semaphore()
    pl.semaphore_signal(barrier, inc=1, device_id={"feat": partner}, device_id_type=MESH)
    each_peer(
        lambda k: pl.semaphore_signal(
            barrier, inc=1, device_id={"dom": peer(k)}, device_id_type=MESH
        )
    )
    keep = (pre_ref[...] > 0).astype(F32)
    cols[half] = (grad_ref[...].astype(F32) * keep).astype(BF16)
    place = (
        lax.broadcasted_iota(jnp.int32, source_ref.shape, 0) * LANES
        + lax.broadcasted_iota(jnp.int32, source_ref.shape, 1)
    )
    live[...] = jnp.where(place < limit_ref[0], source_ref[...], -1)
    asked[me] = wanted_ref[me]
    pl.semaphore_wait(barrier, parts)

    exchange = pltpu.make_async_remote_copy(
        src_ref=cols.at[half],
        dst_ref=cols.at[half],
        send_sem=feat_sems.at[0],
        recv_sem=feat_sems.at[1],
        device_id={"feat": partner},
        device_id_type=MESH,
    )
    exchange.start()

    def request(k):
        return copy(0, k, wanted_ref.at[peer(k)], asked.at[me])

    each_peer(lambda k: request(k).start())
    pltpu.make_async_remote_copy(
        src_ref=cols.at[half],
        dst_ref=cols.at[partner],
        send_sem=feat_sems.at[0],
        recv_sem=feat_sems.at[1],
        device_id={"feat": partner},
        device_id_type=MESH,
    ).wait_recv()

    neigh = dot(cols[0], w_neigh_ref[:, :width], (1, 1)) + dot(
        cols[1], w_neigh_ref[:, width:], (1, 1)
    )
    for g in range(masters // LANES):
        at = slice(g * LANES, (g + 1) * LANES)
        degree = columns_of(degree_ref[g : g + 1, :]).astype(F32)
        degree = jnp.concatenate([degree] * (width // LANES), axis=1)
        table[at, :] = (neigh[at, :] / degree).astype(BF16)

    each_peer(lambda k: copy(0, k, wanted_ref.at[peer(k)], asked.at[giver(k)]).wait_recv())

    def hits(q):
        hub = lax.broadcasted_iota(jnp.int32, (HUBS, slots), 0)
        return jnp.where(hub == asked[q], jnp.ones((), BF16), jnp.zeros((), BF16))

    def answer(k, c):
        q = peer(k)
        replies[rows_of(q), :] = dot(hits(q), table[:HUBS, :], (0, 0)).astype(BF16)
        return c

    lax.fori_loop(0, parts, answer, 0)
    mirrors[rows_of(me), :] = replies[rows_of(me), :]

    def reply(k):
        return copy(1, k, replies.at[rows_of(peer(k)), :], mirrors.at[rows_of(me), :])

    each_peer(lambda k: reply(k).start())

    per_weight = chunks // 2
    for i, operand in enumerate((features_ref, mean_ref)):
        for h in range(2):
            part = dot(operand[...], cols[h], (0, 0)).astype(BF16)
            for c in range(per_weight):
                partial[i * per_weight + c, :, h * width : (h + 1) * width] = part[
                    c * chunk : (c + 1) * chunk, :
                ]

    def guarded(act, owner):
        if chunks == parts:
            return act
        return lambda k: pl.when(owner(k) < chunks)(lambda: act(k))

    def scatter(k):
        return copy(2, k, partial.at[lax.rem(peer(k), chunks)], arrived.at[me])

    each_peer(guarded(lambda k: scatter(k).start(), peer))
    master_sum[...] = dot(cols[0], w_self_ref[:, :width], (1, 1)) + dot(
        cols[1], w_self_ref[:, width:], (1, 1)
    )

    def block_at(b):
        return pl.ds(pl.multiple_of(b * groups, groups), groups)

    def edges_at(b):
        return pl.ds(pl.multiple_of(b * block, block), block)

    def from_masters(b, c):
        pick = pick_rows(sink_ref[block_at(b), :], 0, masters)
        picked[edges_at(b), :] = dot(pick, table[...], (1, 0)).astype(BF16)
        return c

    lax.fori_loop(0, blocks, from_masters, 0)

    each_peer(
        lambda k: copy(
            1, k, replies.at[rows_of(peer(k)), :], mirrors.at[rows_of(giver(k)), :]
        ).wait_recv()
    )
    mirror_sum[...] = jnp.zeros_like(mirror_sum)
    mirror_count = mirrors.shape[0]

    def from_mirrors(b, c):
        pick = pick_rows(sink_ref[block_at(b), :], masters, mirror_count)
        more = dot(pick, mirrors[...], (1, 0)).astype(BF16)
        row = picked[edges_at(b), :] + more
        picked[edges_at(b), :] = row
        put = put_rows(live[block_at(b), :], masters, mirror_count)
        mirror_sum[...] += dot(put, row, (1, 0))
        return c

    lax.fori_loop(0, blocks, from_mirrors, 0)
    returns[...] = mirror_sum[...].astype(BF16)
    returned[rows_of(me), :] = returns[rows_of(me), :]

    def give_back(k):
        return copy(3, k, returns.at[rows_of(peer(k)), :], returned.at[rows_of(me), :])

    each_peer(lambda k: give_back(k).start())

    def reduce_chunk():
        arrived[me] = partial[lax.rem(me, chunks)]
        each_peer(
            lambda k: copy(
                2, k, partial.at[lax.rem(peer(k), chunks)], arrived.at[giver(k)]
            ).wait_recv()
        )
        total = lax.fori_loop(
            0,
            parts,
            lambda p, t: t + arrived[p].astype(F32),
            jnp.zeros(partial.shape[1:], F32),
        )
        summed[lax.rem(me, chunks)] = total.astype(BF16)

    def spread(k):
        return copy(4, k, summed.at[lax.rem(me, chunks)], summed.at[lax.rem(me, chunks)])

    def reduce_and_spread():
        reduce_chunk()
        each_peer(lambda k: spread(k).start())

    if chunks == parts:
        reduce_and_spread()
    else:
        pl.when(me < chunks)(reduce_and_spread)

    def to_masters(b, c):
        put = put_rows(live[block_at(b), :], 0, masters)
        master_sum[...] += dot(put, picked[edges_at(b), :], (1, 0))
        return c

    lax.fori_loop(0, blocks, to_masters, 0)

    each_peer(
        lambda k: copy(
            3, k, returns.at[rows_of(peer(k)), :], returned.at[rows_of(giver(k)), :]
        ).wait_recv()
    )
    hub_sum = lax.fori_loop(
        0,
        parts,
        lambda q, t: t + dot(hits(q), returned[rows_of(q), :], (1, 0)),
        master_sum[:HUBS, :],
    )
    out_ref[:HUBS, :] = hub_sum.astype(BF16)
    out_ref[HUBS:, :] = master_sum[HUBS:, :].astype(BF16)

    each_peer(
        guarded(
            lambda k: copy(
                4,
                k,
                summed.at[lax.rem(me, chunks)],
                summed.at[lax.rem(giver(k), chunks)],
            ).wait_recv(),
            giver,
        )
    )
    weights_ref[...] = summed[...]

    exchange.wait_send()
    each_peer(lambda k: request(k).wait_send())
    each_peer(lambda k: reply(k).wait_send())
    each_peer(guarded(lambda k: scatter(k).wait_send(), peer))
    each_peer(lambda k: give_back(k).wait_send())
    each_peer(guarded(lambda k: spread(k).wait_send(), lambda k: me))


def on_device(
    features,
    grad_out,
    pre_act,
    neigh_mean,
    w_self,
    w_neigh,
    edge_from,
    edge_to,
    edge_count,
    mirror_master,
    degrees,
):
    masters, width = features.shape
    parts = lax.axis_size("dom")
    mirror_count = mirror_master.shape[0]
    slots = mirror_count // parts
    edges = edge_from.shape[0]
    full = w_self.shape[1]
    weight_rows = 2 * w_self.shape[0]
    chunks = min(parts, weight_rows // 16)
    chunk = weight_rows // chunks
    block = min(edges, 1024 if masters + mirror_count <= 2048 else 256)
    vmem = pl.BlockSpec(memory_space=pltpu.VMEM)
    input_grad, weights = pl.pallas_call(
        functools.partial(layer_kernel, parts, block),
        out_shape=(
            jax.ShapeDtypeStruct((masters, width), BF16),
            jax.ShapeDtypeStruct((chunks, chunk, full), BF16),
        ),
        in_specs=[pl.BlockSpec(memory_space=pltpu.SMEM)] + [vmem] * 10,
        out_specs=(vmem, vmem),
        scratch_shapes=[
            pltpu.VMEM((2, masters, width), BF16),
            pltpu.VMEM((edges // LANES, LANES), jnp.int32),
            pltpu.VMEM((masters, width), BF16),
            pltpu.VMEM((parts, 1, slots), jnp.int32),
            pltpu.VMEM((mirror_count, width), BF16),
            pltpu.VMEM((mirror_count, width), BF16),
            pltpu.VMEM((edges, width), BF16),
            pltpu.VMEM((masters, width), F32),
            pltpu.VMEM((mirror_count, width), F32),
            pltpu.VMEM((mirror_count, width), BF16),
            pltpu.VMEM((mirror_count, width), BF16),
            pltpu.VMEM((chunks, chunk, full), BF16),
            pltpu.VMEM((parts, chunk, full), BF16),
            pltpu.VMEM((chunks, chunk, full), BF16),
            pltpu.SemaphoreType.DMA((2,)),
            pltpu.SemaphoreType.DMA((5, parts)),
            pltpu.SemaphoreType.DMA((5, parts)),
        ],
        compiler_params=pltpu.CompilerParams(
            collective_id=0, has_side_effects=True, vmem_limit_bytes=60 * 2**20
        ),
    )(
        edge_count,
        grad_out,
        pre_act,
        features,
        neigh_mean,
        w_self,
        w_neigh,
        edge_from.reshape(-1, LANES),
        edge_to.reshape(-1, LANES),
        mirror_master.reshape(parts, 1, slots),
        degrees.reshape(-1, LANES),
    )
    weights = weights.reshape(2, w_self.shape[0], full).astype(F32)
    return (input_grad, weights[0], weights[1])


def solution(mesh):
    placed = (
        P("dom", "feat"),
        P("dom", "feat"),
        P("dom", "feat"),
        P("dom", "feat"),
        P("feat", None),
        P("feat", None),
        P("dom"),
        P("dom"),
        P("dom"),
        P("dom"),
        P("dom"),
    )
    return jax.shard_map(
        on_device,
        mesh=mesh,
        in_specs=placed,
        out_specs=(P("dom", "feat"), P("feat", None), P("feat", None)),
        check_vma=False,
    )
```

```python
import functools

import jax
import jax.numpy as jnp
from jax import lax
from jax.experimental import pallas as pl
from jax.experimental.pallas import tpu as pltpu
from jax.sharding import PartitionSpec as P

LANES = 128
HUBS = 64
MESH = pl.DeviceIdType.MESH
F32, BF16 = jnp.float32, jnp.bfloat16


def dot(a, b, over):
    return lax.dot_general(a, b, ((over[:1], over[1:]), ((), ())), preferred_element_type=F32)


def columns_of(row):
    return jnp.transpose(jnp.broadcast_to(row, (LANES, LANES)))


def pick_rows(sinks, first, count):
    one, zero = jnp.ones((), BF16), jnp.zeros((), BF16)
    lane = lax.broadcasted_iota(jnp.int32, (LANES, LANES), 1)
    tiles = []
    for g in range(sinks.shape[0]):
        column = columns_of(sinks[g : g + 1, :])
        tiles.append(
            jnp.concatenate(
                [jnp.where(column == lane + (first + j), one, zero) for j in range(0, count, LANES)],
                axis=1,
            )
        )
    return jnp.concatenate(tiles, axis=0)


def put_rows(sources, first, count):
    one, zero = jnp.ones((), BF16), jnp.zeros((), BF16)
    row = lax.broadcasted_iota(jnp.int32, (count, LANES), 0) + first
    return jnp.concatenate(
        [jnp.where(row == sources[g : g + 1, :], one, zero) for g in range(sources.shape[0])],
        axis=1,
    )


def layer_kernel(
    parts,
    block,
    limit_ref,
    grad_ref,
    pre_ref,
    features_hbm,
    mean_hbm,
    w_self_hbm,
    w_neigh_hbm,
    source_ref,
    sink_ref,
    wanted_ref,
    degree_ref,
    out_ref,
    weights_ref,
    features_ref,
    mean_ref,
    w_self_ref,
    w_neigh_ref,
    cols,
    live,
    table,
    asked,
    replies,
    mirrors,
    picked,
    master_sum,
    mirror_sum,
    returns,
    returned,
    hits,
    partial,
    arrived,
    column_sum,
    column_arrived,
    column_total,
    full,
    load_sems,
    feat_sems,
    send_sems,
    recv_sems,
):
    me, half = lax.axis_index("dom"), lax.axis_index("feat")
    partner = 1 - half
    masters, width = grad_ref.shape
    slots = wanted_ref.shape[2]
    low, low_rows = partial.shape[0], partial.shape[1]
    owners, chunk = column_sum.shape[0], column_sum.shape[1]
    high = parts // low
    at_high, at_low = me // low, lax.rem(me, low)
    groups = block // LANES
    blocks = sink_ref.shape[0] // groups

    def peer(k):
        return lax.rem(me + k, parts)

    def giver(k):
        return lax.rem(me + (parts - k), parts)

    def rows_of(q):
        return pl.ds(pl.multiple_of(q * slots, slots), slots)

    def copy(stage, k, src, dst, device=None):
        return pltpu.make_async_remote_copy(
            src_ref=src,
            dst_ref=dst,
            send_sem=send_sems.at[stage, k],
            recv_sem=recv_sems.at[stage, k],
            device_id={"dom": peer(k) if device is None else device},
            device_id_type=MESH,
        )

    def each_peer(act, count=parts):
        lax.fori_loop(1, count, lambda k, c: (act(k), c)[1], 0)

    loads = [
        pltpu.make_async_copy(src, dst, load_sems.at[i])
        for i, (src, dst) in enumerate(
            (
                (w_neigh_hbm, w_neigh_ref),
                (features_hbm, features_ref),
                (mean_hbm, mean_ref),
                (w_self_hbm, w_self_ref),
            )
        )
    ]

    barrier = pltpu.get_barrier_semaphore()
    pl.semaphore_signal(barrier, inc=1, device_id={"feat": partner}, device_id_type=MESH)
    each_peer(
        lambda k: pl.semaphore_signal(
            barrier, inc=1, device_id={"dom": peer(k)}, device_id_type=MESH
        )
    )
    for load in loads:
        load.start()
    keep = (pre_ref[...] > 0).astype(F32)
    cols[half] = (grad_ref[...].astype(F32) * keep).astype(BF16)
    place = (
        lax.broadcasted_iota(jnp.int32, source_ref.shape, 0) * LANES
        + lax.broadcasted_iota(jnp.int32, source_ref.shape, 1)
    )
    live[...] = jnp.where(place < limit_ref[0], source_ref[...], -1)
    asked[me] = wanted_ref[me]
    pl.semaphore_wait(barrier, parts)

    exchange = pltpu.make_async_remote_copy(
        src_ref=cols.at[half],
        dst_ref=cols.at[half],
        send_sem=feat_sems.at[0],
        recv_sem=feat_sems.at[1],
        device_id={"feat": partner},
        device_id_type=MESH,
    )
    exchange.start()

    def request(k):
        return copy(0, k, wanted_ref.at[peer(k)], asked.at[me])

    each_peer(lambda k: request(k).start())
    pltpu.make_async_remote_copy(
        src_ref=cols.at[half],
        dst_ref=cols.at[partner],
        send_sem=feat_sems.at[0],
        recv_sem=feat_sems.at[1],
        device_id={"feat": partner},
        device_id_type=MESH,
    ).wait_recv()

    loads[0].wait()
    neigh = dot(cols[0], w_neigh_ref[:, :width], (1, 1)) + dot(
        cols[1], w_neigh_ref[:, width:], (1, 1)
    )
    for g in range(masters // LANES):
        at = slice(g * LANES, (g + 1) * LANES)
        degree = columns_of(degree_ref[g : g + 1, :]).astype(F32)
        degree = jnp.concatenate([degree] * (width // LANES), axis=1)
        table[at, :] = (neigh[at, :] / degree).astype(BF16)

    each_peer(lambda k: copy(0, k, wanted_ref.at[peer(k)], asked.at[giver(k)]).wait_recv())

    batch = 8 if parts % 8 == 0 else 1
    hub = lax.broadcasted_iota(jnp.int32, (HUBS, slots), 0)

    def batch_at(i):
        return pl.ds(pl.multiple_of(i * batch * slots, batch * slots), batch * slots)

    def answer(i, c):
        hit = jnp.concatenate(
            [
                jnp.where(hub == asked[i * batch + j], jnp.ones((), BF16), jnp.zeros((), BF16))
                for j in range(batch)
            ],
            axis=1,
        )
        hits[i] = hit
        replies[batch_at(i), :] = dot(hit, table[:HUBS, :], (0, 0)).astype(BF16)
        return c

    lax.fori_loop(0, parts // batch, answer, 0)
    mirrors[rows_of(me), :] = replies[rows_of(me), :]

    def reply(k):
        return copy(1, k, replies.at[rows_of(peer(k)), :], mirrors.at[rows_of(me), :])

    each_peer(lambda k: reply(k).start())

    both = jnp.concatenate([cols[0], cols[1]], axis=1)
    per_weight = low // 2
    for i, operand in enumerate((features_ref, mean_ref)):
        loads[1 + i].wait()
        part = dot(operand[...], both, (0, 0)).astype(BF16)
        for c in range(per_weight):
            partial[i * per_weight + c] = part[c * low_rows : (c + 1) * low_rows, :]

    def low_peer(k):
        return lax.rem(at_low + k, low)

    def low_giver(k):
        return lax.rem(at_low + (low - k), low)

    def high_peer(k):
        return lax.rem(at_high + k, high)

    def high_giver(k):
        return lax.rem(at_high + (high - k), high)

    def to_low(stage, k, src, dst):
        return copy(stage, k, src, dst, at_high * low + low_peer(k))

    def to_high(stage, k, src, dst):
        return copy(stage, k, src, dst, high_peer(k) * low + at_low)

    def guarded(act, owner):
        if owners == high:
            return act
        return lambda k: pl.when(owner(k) < owners)(lambda: act(k))

    def if_owner(act):
        if owners == high:
            act()
        else:
            pl.when(at_high < owners)(act)

    def scatter(k):
        return to_low(2, k, partial.at[low_peer(k)], arrived.at[at_low])

    each_peer(lambda k: scatter(k).start(), low)
    loads[3].wait()
    master_sum[...] = dot(cols[0], w_self_ref[:, :width], (1, 1)) + dot(
        cols[1], w_self_ref[:, width:], (1, 1)
    )

    def block_at(b):
        return pl.ds(pl.multiple_of(b * groups, groups), groups)

    def edges_at(b):
        return pl.ds(pl.multiple_of(b * block, block), block)

    def from_masters(b, c):
        pick = pick_rows(sink_ref[block_at(b), :], 0, masters)
        picked[edges_at(b), :] = dot(pick, table[...], (1, 0)).astype(BF16)
        return c

    lax.fori_loop(0, blocks, from_masters, 0)

    each_peer(
        lambda k: to_low(2, k, partial.at[low_peer(k)], arrived.at[low_giver(k)]).wait_recv(), low
    )
    total = lax.fori_loop(
        1,
        low,
        lambda k, t: t + arrived[low_giver(k)].astype(F32),
        partial[at_low].astype(F32),
    ).astype(BF16)
    for c in range(owners):
        column_sum[c] = total[c * chunk : (c + 1) * chunk, :]

    def column_place():
        return lax.rem(at_high, owners)

    def scatter_high(k):
        return to_high(
            4, k, column_sum.at[lax.rem(high_peer(k), owners)], column_arrived.at[at_high]
        )

    each_peer(guarded(lambda k: scatter_high(k).start(), high_peer), high)

    each_peer(
        lambda k: copy(
            1, k, replies.at[rows_of(peer(k)), :], mirrors.at[rows_of(giver(k)), :]
        ).wait_recv()
    )
    mirror_sum[...] = jnp.zeros_like(mirror_sum)
    mirror_count = mirrors.shape[0]

    def from_mirrors(b, c):
        pick = pick_rows(sink_ref[block_at(b), :], masters, mirror_count)
        more = dot(pick, mirrors[...], (1, 0)).astype(BF16)
        row = picked[edges_at(b), :] + more
        picked[edges_at(b), :] = row
        return c

    lax.fori_loop(0, blocks, from_mirrors, 0)

    def to_mirrors(b, c):
        put = put_rows(live[block_at(b), :], masters, mirror_count)
        mirror_sum[...] += dot(put, picked[edges_at(b), :], (1, 0))
        return c

    lax.fori_loop(0, blocks, to_mirrors, 0)
    returns[...] = mirror_sum[...].astype(BF16)
    returned[rows_of(me), :] = returns[rows_of(me), :]

    def give_back(k):
        return copy(3, k, returns.at[rows_of(peer(k)), :], returned.at[rows_of(me), :])

    each_peer(lambda k: give_back(k).start())

    def column_spread(k):
        return to_high(5, k, column_total.at[column_place()], column_total.at[column_place()])

    def reduce_column():
        each_peer(
            lambda k: to_high(
                4,
                k,
                column_sum.at[lax.rem(high_peer(k), owners)],
                column_arrived.at[high_giver(k)],
            ).wait_recv(),
            high,
        )
        column_total[column_place()] = lax.fori_loop(
            1,
            high,
            lambda k, t: t + column_arrived[high_giver(k)].astype(F32),
            column_sum[column_place()].astype(F32),
        ).astype(BF16)
        each_peer(lambda k: column_spread(k).start(), high)

    if_owner(reduce_column)

    def to_masters(b, c):
        put = put_rows(live[block_at(b), :], 0, masters)
        master_sum[...] += dot(put, picked[edges_at(b), :], (1, 0))
        return c

    early = blocks // 2
    lax.fori_loop(0, early, to_masters, 0)

    each_peer(
        guarded(
            lambda k: to_high(
                5,
                k,
                column_total.at[column_place()],
                column_total.at[lax.rem(high_giver(k), owners)],
            ).wait_recv(),
            high_giver,
        ),
        high,
    )
    full[at_low] = column_total[...]

    def spread(k):
        return to_low(6, k, column_total, full.at[at_low])

    each_peer(lambda k: spread(k).start(), low)
    lax.fori_loop(early, blocks, to_masters, 0)

    each_peer(
        lambda k: copy(
            3, k, returns.at[rows_of(peer(k)), :], returned.at[rows_of(giver(k)), :]
        ).wait_recv()
    )
    hub_sum = lax.fori_loop(
        0,
        parts // batch,
        lambda i, t: t + dot(hits[i], returned[batch_at(i), :], (1, 0)),
        master_sum[:HUBS, :],
    )
    out_ref[:HUBS, :] = hub_sum.astype(BF16)
    out_ref[HUBS:, :] = master_sum[HUBS:, :].astype(BF16)

    each_peer(lambda k: to_low(6, k, column_total, full.at[low_giver(k)]).wait_recv(), low)
    weights_ref[...] = full[...]

    exchange.wait_send()
    each_peer(lambda k: request(k).wait_send())
    each_peer(lambda k: reply(k).wait_send())
    each_peer(lambda k: give_back(k).wait_send())
    each_peer(lambda k: scatter(k).wait_send(), low)
    each_peer(guarded(lambda k: scatter_high(k).wait_send(), high_peer), high)
    if_owner(lambda: each_peer(lambda k: column_spread(k).wait_send(), high))
    each_peer(lambda k: spread(k).wait_send(), low)


def on_device(
    features,
    grad_out,
    pre_act,
    neigh_mean,
    w_self,
    w_neigh,
    edge_from,
    edge_to,
    edge_count,
    mirror_master,
    degrees,
):
    masters, width = features.shape
    parts = lax.axis_size("dom")
    mirror_count = mirror_master.shape[0]
    slots = mirror_count // parts
    edges = edge_from.shape[0]
    full = w_self.shape[1]
    weight_rows = 2 * w_self.shape[0]
    low = 2
    while parts % (4 * low) == 0 and 4 * low * low <= parts:
        low *= 2
    low_rows = weight_rows // low
    owners = min(parts // low, low_rows // 16)
    chunk = low_rows // owners
    batch = 8 if parts % 8 == 0 else 1
    block = min(edges, 2048 if masters + mirror_count <= 2048 else 256)
    vmem = pl.BlockSpec(memory_space=pltpu.VMEM)
    anywhere = pl.BlockSpec(memory_space=pl.ANY)
    input_grad, weights = pl.pallas_call(
        functools.partial(layer_kernel, parts, block),
        out_shape=(
            jax.ShapeDtypeStruct((masters, width), BF16),
            jax.ShapeDtypeStruct((low, owners, chunk, full), BF16),
        ),
        in_specs=[pl.BlockSpec(memory_space=pltpu.SMEM)] + [vmem] * 2 + [anywhere] * 4 + [vmem] * 4,
        out_specs=(vmem, vmem),
        scratch_shapes=[
            pltpu.VMEM(features.shape, BF16),
            pltpu.VMEM(features.shape, BF16),
            pltpu.VMEM(w_self.shape, BF16),
            pltpu.VMEM(w_self.shape, BF16),
            pltpu.VMEM((2, masters, width), BF16),
            pltpu.VMEM((edges // LANES, LANES), jnp.int32),
            pltpu.VMEM((masters, width), BF16),
            pltpu.VMEM((parts, 1, slots), jnp.int32),
            pltpu.VMEM((mirror_count, width), BF16),
            pltpu.VMEM((mirror_count, width), BF16),
            pltpu.VMEM((edges, width), BF16),
            pltpu.VMEM((masters, width), F32),
            pltpu.VMEM((mirror_count, width), F32),
            pltpu.VMEM((mirror_count, width), BF16),
            pltpu.VMEM((mirror_count, width), BF16),
            pltpu.VMEM((parts // batch, HUBS, batch * slots), BF16),
            pltpu.VMEM((low, low_rows, full), BF16),
            pltpu.VMEM((low, low_rows, full), BF16),
            pltpu.VMEM((owners, chunk, full), BF16),
            pltpu.VMEM((parts // low, chunk, full), BF16),
            pltpu.VMEM((owners, chunk, full), BF16),
            pltpu.VMEM((low, owners, chunk, full), BF16),
            pltpu.SemaphoreType.DMA((4,)),
            pltpu.SemaphoreType.DMA((2,)),
            pltpu.SemaphoreType.DMA((7, parts)),
            pltpu.SemaphoreType.DMA((7, parts)),
        ],
        compiler_params=pltpu.CompilerParams(
            collective_id=0, has_side_effects=True, vmem_limit_bytes=60 * 2**20
        ),
    )(
        edge_count,
        grad_out,
        pre_act,
        features,
        neigh_mean,
        w_self,
        w_neigh,
        edge_from.reshape(-1, LANES),
        edge_to.reshape(-1, LANES),
        mirror_master.reshape(parts, 1, slots),
        degrees.reshape(-1, LANES),
    )
    weights = weights.reshape(2, w_self.shape[0], full).astype(F32)
    return (input_grad, weights[0], weights[1])


def solution(mesh):
    placed = (
        P("dom", "feat"),
        P("dom", "feat"),
        P("dom", "feat"),
        P("dom", "feat"),
        P("feat", None),
        P("feat", None),
        P("dom"),
        P("dom"),
        P("dom"),
        P("dom"),
        P("dom"),
    )
    return jax.shard_map(
        on_device,
        mesh=mesh,
        in_specs=placed,
        out_specs=(P("dom", "feat"), P("feat", None), P("feat", None)),
        check_vma=False,
    )
```

```python
import functools

import jax
import jax.numpy as jnp
from jax import lax
from jax.experimental import pallas as pl
from jax.experimental.pallas import tpu as pltpu
from jax.sharding import PartitionSpec as P

LANES = 128
HUBS = 64
MESH = pl.DeviceIdType.MESH
F32, BF16 = jnp.float32, jnp.bfloat16


def dot(a, b, over):
    return lax.dot_general(a, b, ((over[:1], over[1:]), ((), ())), preferred_element_type=F32)


def columns_of(row):
    return jnp.transpose(jnp.broadcast_to(row, (LANES, LANES)))


def pick_rows(sinks, first, count):
    one, zero = jnp.ones((), BF16), jnp.zeros((), BF16)
    lane = lax.broadcasted_iota(jnp.int32, (LANES, LANES), 1)
    tiles = []
    for g in range(sinks.shape[0]):
        column = columns_of(sinks[g : g + 1, :])
        tiles.append(
            jnp.concatenate(
                [jnp.where(column == lane + (first + j), one, zero) for j in range(0, count, LANES)],
                axis=1,
            )
        )
    return jnp.concatenate(tiles, axis=0)


def put_rows(sources, first, count):
    one, zero = jnp.ones((), BF16), jnp.zeros((), BF16)
    row = lax.broadcasted_iota(jnp.int32, (count, LANES), 0) + first
    return jnp.concatenate(
        [jnp.where(row == sources[g : g + 1, :], one, zero) for g in range(sources.shape[0])],
        axis=1,
    )


def layer_kernel(
    parts,
    block,
    limit_ref,
    grad_ref,
    pre_ref,
    features_hbm,
    mean_hbm,
    w_self_hbm,
    w_neigh_hbm,
    source_ref,
    sink_ref,
    wanted_ref,
    degree_ref,
    out_ref,
    weights_ref,
    features_ref,
    mean_ref,
    w_self_ref,
    w_neigh_ref,
    cols,
    live,
    table,
    asked,
    replies,
    mirrors,
    picked,
    master_sum,
    mirror_sum,
    returns,
    returned,
    hits,
    partial,
    arrived,
    column_sum,
    column_arrived,
    column_total,
    full,
    load_sems,
    feat_sems,
    send_sems,
    recv_sems,
):
    me, half = lax.axis_index("dom"), lax.axis_index("feat")
    partner = 1 - half
    masters, width = grad_ref.shape
    slots = wanted_ref.shape[2]
    low, low_rows = partial.shape[0], partial.shape[1]
    owners, chunk = column_sum.shape[0], column_sum.shape[1]
    high = parts // low
    at_high, at_low = me // low, lax.rem(me, low)
    groups = block // LANES
    blocks = sink_ref.shape[0] // groups

    def peer(k):
        return lax.rem(me + k, parts)

    def giver(k):
        return lax.rem(me + (parts - k), parts)

    def rows_of(q):
        return pl.ds(pl.multiple_of(q * slots, slots), slots)

    def copy(stage, k, src, dst, device=None):
        return pltpu.make_async_remote_copy(
            src_ref=src,
            dst_ref=dst,
            send_sem=send_sems.at[stage, k],
            recv_sem=recv_sems.at[stage, k],
            device_id={"dom": peer(k) if device is None else device},
            device_id_type=MESH,
        )

    def each_peer(act, count=parts):
        lax.fori_loop(1, count, lambda k, c: (act(k), c)[1], 0)

    loads = [
        pltpu.make_async_copy(src, dst, load_sems.at[i])
        for i, (src, dst) in enumerate(
            (
                (w_neigh_hbm, w_neigh_ref),
                (features_hbm, features_ref),
                (mean_hbm, mean_ref),
                (w_self_hbm, w_self_ref),
            )
        )
    ]

    barrier = pltpu.get_barrier_semaphore()
    pl.semaphore_signal(barrier, inc=1, device_id={"feat": partner}, device_id_type=MESH)
    each_peer(
        lambda k: pl.semaphore_signal(
            barrier, inc=1, device_id={"dom": peer(k)}, device_id_type=MESH
        )
    )
    for load in loads:
        load.start()
    keep = (pre_ref[...] > 0).astype(F32)
    cols[half] = (grad_ref[...].astype(F32) * keep).astype(BF16)
    place = (
        lax.broadcasted_iota(jnp.int32, source_ref.shape, 0) * LANES
        + lax.broadcasted_iota(jnp.int32, source_ref.shape, 1)
    )
    live[...] = jnp.where(place < limit_ref[0], source_ref[...], -1)
    asked[me] = wanted_ref[me]
    pl.semaphore_wait(barrier, parts)

    exchange = pltpu.make_async_remote_copy(
        src_ref=cols.at[half],
        dst_ref=cols.at[half],
        send_sem=feat_sems.at[0],
        recv_sem=feat_sems.at[1],
        device_id={"feat": partner},
        device_id_type=MESH,
    )
    exchange.start()

    def request(k):
        return copy(0, k, wanted_ref.at[peer(k)], asked.at[me])

    each_peer(lambda k: request(k).start())
    pltpu.make_async_remote_copy(
        src_ref=cols.at[half],
        dst_ref=cols.at[partner],
        send_sem=feat_sems.at[0],
        recv_sem=feat_sems.at[1],
        device_id={"feat": partner},
        device_id_type=MESH,
    ).wait_recv()

    both = jnp.concatenate([cols[0], cols[1]], axis=1)
    per_weight = low // 2
    for i, operand in enumerate((features_ref, mean_ref)):
        loads[1 + i].wait()
        part = dot(operand[...], both, (0, 0)).astype(BF16)
        for c in range(per_weight):
            partial[i * per_weight + c] = part[c * low_rows : (c + 1) * low_rows, :]

    def low_peer(k):
        return lax.rem(at_low + k, low)

    def low_giver(k):
        return lax.rem(at_low + (low - k), low)

    def high_peer(k):
        return lax.rem(at_high + k, high)

    def high_giver(k):
        return lax.rem(at_high + (high - k), high)

    def to_low(stage, k, src, dst):
        return copy(stage, k, src, dst, at_high * low + low_peer(k))

    def to_high(stage, k, src, dst):
        return copy(stage, k, src, dst, high_peer(k) * low + at_low)

    def guarded(act, owner):
        if owners == high:
            return act
        return lambda k: pl.when(owner(k) < owners)(lambda: act(k))

    def if_owner(act):
        if owners == high:
            act()
        else:
            pl.when(at_high < owners)(act)

    def scatter(k):
        return to_low(2, k, partial.at[low_peer(k)], arrived.at[at_low])

    each_peer(lambda k: scatter(k).start(), low)
    loads[0].wait()
    neigh = dot(cols[0], w_neigh_ref[:, :width], (1, 1)) + dot(
        cols[1], w_neigh_ref[:, width:], (1, 1)
    )
    for g in range(masters // LANES):
        at = slice(g * LANES, (g + 1) * LANES)
        degree = columns_of(degree_ref[g : g + 1, :]).astype(F32)
        degree = jnp.concatenate([degree] * (width // LANES), axis=1)
        table[at, :] = (neigh[at, :] / degree).astype(BF16)

    each_peer(lambda k: copy(0, k, wanted_ref.at[peer(k)], asked.at[giver(k)]).wait_recv())

    batch = 8 if parts % 8 == 0 else 1
    hub = lax.broadcasted_iota(jnp.int32, (HUBS, slots), 0)

    def batch_at(i):
        return pl.ds(pl.multiple_of(i * batch * slots, batch * slots), batch * slots)

    def answer(i, c):
        hit = jnp.concatenate(
            [
                jnp.where(hub == asked[i * batch + j], jnp.ones((), BF16), jnp.zeros((), BF16))
                for j in range(batch)
            ],
            axis=1,
        )
        hits[i] = hit
        replies[batch_at(i), :] = dot(hit, table[:HUBS, :], (0, 0)).astype(BF16)
        return c

    lax.fori_loop(0, parts // batch, answer, 0)
    mirrors[rows_of(me), :] = replies[rows_of(me), :]

    def reply(k):
        return copy(1, k, replies.at[rows_of(peer(k)), :], mirrors.at[rows_of(me), :])

    each_peer(lambda k: reply(k).start())

    loads[3].wait()
    master_sum[...] = dot(cols[0], w_self_ref[:, :width], (1, 1)) + dot(
        cols[1], w_self_ref[:, width:], (1, 1)
    )

    def block_at(b):
        return pl.ds(pl.multiple_of(b * groups, groups), groups)

    def edges_at(b):
        return pl.ds(pl.multiple_of(b * block, block), block)

    def from_masters(b, c):
        pick = pick_rows(sink_ref[block_at(b), :], 0, masters)
        picked[edges_at(b), :] = dot(pick, table[...], (1, 0)).astype(BF16)
        return c

    lax.fori_loop(0, blocks, from_masters, 0)

    each_peer(
        lambda k: to_low(2, k, partial.at[low_peer(k)], arrived.at[low_giver(k)]).wait_recv(), low
    )
    total = lax.fori_loop(
        1,
        low,
        lambda k, t: t + arrived[low_giver(k)].astype(F32),
        partial[at_low].astype(F32),
    ).astype(BF16)
    for c in range(owners):
        column_sum[c] = total[c * chunk : (c + 1) * chunk, :]

    def column_place():
        return lax.rem(at_high, owners)

    def scatter_high(k):
        return to_high(
            4, k, column_sum.at[lax.rem(high_peer(k), owners)], column_arrived.at[at_high]
        )

    each_peer(guarded(lambda k: scatter_high(k).start(), high_peer), high)

    each_peer(
        lambda k: copy(
            1, k, replies.at[rows_of(peer(k)), :], mirrors.at[rows_of(giver(k)), :]
        ).wait_recv()
    )
    mirror_sum[...] = jnp.zeros_like(mirror_sum)
    mirror_count = mirrors.shape[0]

    def from_mirrors(b, c):
        pick = pick_rows(sink_ref[block_at(b), :], masters, mirror_count)
        more = dot(pick, mirrors[...], (1, 0)).astype(BF16)
        row = picked[edges_at(b), :] + more
        picked[edges_at(b), :] = row
        return c

    lax.fori_loop(0, blocks, from_mirrors, 0)

    def column_spread(k):
        return to_high(5, k, column_total.at[column_place()], column_total.at[column_place()])

    def reduce_column():
        each_peer(
            lambda k: to_high(
                4,
                k,
                column_sum.at[lax.rem(high_peer(k), owners)],
                column_arrived.at[high_giver(k)],
            ).wait_recv(),
            high,
        )
        column_total[column_place()] = lax.fori_loop(
            1,
            high,
            lambda k, t: t + column_arrived[high_giver(k)].astype(F32),
            column_sum[column_place()].astype(F32),
        ).astype(BF16)
        each_peer(lambda k: column_spread(k).start(), high)

    if_owner(reduce_column)

    def to_mirrors(b, c):
        put = put_rows(live[block_at(b), :], masters, mirror_count)
        mirror_sum[...] += dot(put, picked[edges_at(b), :], (1, 0))
        return c

    lax.fori_loop(0, blocks, to_mirrors, 0)
    returns[...] = mirror_sum[...].astype(BF16)
    returned[rows_of(me), :] = returns[rows_of(me), :]

    def give_back(k):
        return copy(3, k, returns.at[rows_of(peer(k)), :], returned.at[rows_of(me), :])

    each_peer(lambda k: give_back(k).start())

    each_peer(
        guarded(
            lambda k: to_high(
                5,
                k,
                column_total.at[column_place()],
                column_total.at[lax.rem(high_giver(k), owners)],
            ).wait_recv(),
            high_giver,
        ),
        high,
    )
    full[at_low] = column_total[...]

    def spread(k):
        return to_low(6, k, column_total, full.at[at_low])

    each_peer(lambda k: spread(k).start(), low)

    def to_masters(b, c):
        put = put_rows(live[block_at(b), :], 0, masters)
        master_sum[...] += dot(put, picked[edges_at(b), :], (1, 0))
        return c

    lax.fori_loop(0, blocks, to_masters, 0)

    each_peer(
        lambda k: copy(
            3, k, returns.at[rows_of(peer(k)), :], returned.at[rows_of(giver(k)), :]
        ).wait_recv()
    )
    hub_sum = lax.fori_loop(
        0,
        parts // batch,
        lambda i, t: t + dot(hits[i], returned[batch_at(i), :], (1, 0)),
        master_sum[:HUBS, :],
    )
    out_ref[:HUBS, :] = hub_sum.astype(BF16)
    out_ref[HUBS:, :] = master_sum[HUBS:, :].astype(BF16)

    each_peer(lambda k: to_low(6, k, column_total, full.at[low_giver(k)]).wait_recv(), low)
    weights_ref[...] = full[...]

    exchange.wait_send()
    each_peer(lambda k: request(k).wait_send())
    each_peer(lambda k: reply(k).wait_send())
    each_peer(lambda k: give_back(k).wait_send())
    each_peer(lambda k: scatter(k).wait_send(), low)
    each_peer(guarded(lambda k: scatter_high(k).wait_send(), high_peer), high)
    if_owner(lambda: each_peer(lambda k: column_spread(k).wait_send(), high))
    each_peer(lambda k: spread(k).wait_send(), low)


def on_device(
    features,
    grad_out,
    pre_act,
    neigh_mean,
    w_self,
    w_neigh,
    edge_from,
    edge_to,
    edge_count,
    mirror_master,
    degrees,
):
    masters, width = features.shape
    parts = lax.axis_size("dom")
    mirror_count = mirror_master.shape[0]
    slots = mirror_count // parts
    edges = edge_from.shape[0]
    full = w_self.shape[1]
    weight_rows = 2 * w_self.shape[0]
    low = 2
    while parts % (4 * low) == 0 and 4 * low * low <= parts:
        low *= 2
    low_rows = weight_rows // low
    owners = min(parts // low, low_rows // 16)
    chunk = low_rows // owners
    batch = 8 if parts % 8 == 0 else 1
    block = min(edges, 2048 if masters + mirror_count <= 2048 else 256)
    vmem = pl.BlockSpec(memory_space=pltpu.VMEM)
    anywhere = pl.BlockSpec(memory_space=pl.ANY)
    input_grad, weights = pl.pallas_call(
        functools.partial(layer_kernel, parts, block),
        out_shape=(
            jax.ShapeDtypeStruct((masters, width), BF16),
            jax.ShapeDtypeStruct((low, owners, chunk, full), BF16),
        ),
        in_specs=[pl.BlockSpec(memory_space=pltpu.SMEM)] + [vmem] * 2 + [anywhere] * 4 + [vmem] * 4,
        out_specs=(vmem, vmem),
        scratch_shapes=[
            pltpu.VMEM(features.shape, BF16),
            pltpu.VMEM(features.shape, BF16),
            pltpu.VMEM(w_self.shape, BF16),
            pltpu.VMEM(w_self.shape, BF16),
            pltpu.VMEM((2, masters, width), BF16),
            pltpu.VMEM((edges // LANES, LANES), jnp.int32),
            pltpu.VMEM((masters, width), BF16),
            pltpu.VMEM((parts, 1, slots), jnp.int32),
            pltpu.VMEM((mirror_count, width), BF16),
            pltpu.VMEM((mirror_count, width), BF16),
            pltpu.VMEM((edges, width), BF16),
            pltpu.VMEM((masters, width), F32),
            pltpu.VMEM((mirror_count, width), F32),
            pltpu.VMEM((mirror_count, width), BF16),
            pltpu.VMEM((mirror_count, width), BF16),
            pltpu.VMEM((parts // batch, HUBS, batch * slots), BF16),
            pltpu.VMEM((low, low_rows, full), BF16),
            pltpu.VMEM((low, low_rows, full), BF16),
            pltpu.VMEM((owners, chunk, full), BF16),
            pltpu.VMEM((parts // low, chunk, full), BF16),
            pltpu.VMEM((owners, chunk, full), BF16),
            pltpu.VMEM((low, owners, chunk, full), BF16),
            pltpu.SemaphoreType.DMA((4,)),
            pltpu.SemaphoreType.DMA((2,)),
            pltpu.SemaphoreType.DMA((7, parts)),
            pltpu.SemaphoreType.DMA((7, parts)),
        ],
        compiler_params=pltpu.CompilerParams(
            collective_id=0, has_side_effects=True, vmem_limit_bytes=60 * 2**20
        ),
    )(
        edge_count,
        grad_out,
        pre_act,
        features,
        neigh_mean,
        w_self,
        w_neigh,
        edge_from.reshape(-1, LANES),
        edge_to.reshape(-1, LANES),
        mirror_master.reshape(parts, 1, slots),
        degrees.reshape(-1, LANES),
    )
    weights = weights.reshape(2, w_self.shape[0], full).astype(F32)
    return (input_grad, weights[0], weights[1])


def solution(mesh):
    placed = (
        P("dom", "feat"),
        P("dom", "feat"),
        P("dom", "feat"),
        P("dom", "feat"),
        P("feat", None),
        P("feat", None),
        P("dom"),
        P("dom"),
        P("dom"),
        P("dom"),
        P("dom"),
    )
    return jax.shard_map(
        on_device,
        mesh=mesh,
        in_specs=placed,
        out_specs=(P("dom", "feat"), P("feat", None), P("feat", None)),
        check_vma=False,
    )
```

```python
import functools

import jax
import jax.numpy as jnp
from jax import lax
from jax.experimental import pallas as pl
from jax.experimental.pallas import tpu as pltpu
from jax.sharding import PartitionSpec as P

LANES = 128
HUBS = 64
MESH = pl.DeviceIdType.MESH
F32, BF16 = jnp.float32, jnp.bfloat16


def dot(a, b, over):
    return lax.dot_general(a, b, ((over[:1], over[1:]), ((), ())), preferred_element_type=F32)


def columns_of(row):
    return jnp.transpose(jnp.broadcast_to(row, (LANES, LANES)))


def pick_rows(sinks, first, count):
    one, zero = jnp.ones((), BF16), jnp.zeros((), BF16)
    lane = lax.broadcasted_iota(jnp.int32, (LANES, LANES), 1)
    tiles = []
    for g in range(sinks.shape[0]):
        column = columns_of(sinks[g : g + 1, :])
        tiles.append(
            jnp.concatenate(
                [jnp.where(column == lane + (first + j), one, zero) for j in range(0, count, LANES)],
                axis=1,
            )
        )
    return jnp.concatenate(tiles, axis=0)


def put_rows(sources, first, count):
    one, zero = jnp.ones((), BF16), jnp.zeros((), BF16)
    row = lax.broadcasted_iota(jnp.int32, (count, LANES), 0) + first
    return jnp.concatenate(
        [jnp.where(row == sources[g : g + 1, :], one, zero) for g in range(sources.shape[0])],
        axis=1,
    )


def layer_kernel(
    parts,
    block,
    limit_ref,
    grad_ref,
    pre_ref,
    features_hbm,
    mean_hbm,
    w_self_hbm,
    w_neigh_hbm,
    source_ref,
    sink_ref,
    wanted_ref,
    degree_ref,
    out_ref,
    weights_ref,
    features_ref,
    mean_ref,
    w_self_ref,
    w_neigh_ref,
    cols,
    live,
    table,
    asked,
    replies,
    mirrors,
    picked,
    master_sum,
    mirror_sum,
    returns,
    returned,
    hits,
    partial,
    arrived,
    column_sum,
    column_arrived,
    column_total,
    full,
    load_sems,
    feat_sems,
    send_sems,
    recv_sems,
):
    me, half = lax.axis_index("dom"), lax.axis_index("feat")
    partner = 1 - half
    masters, width = grad_ref.shape
    slots = wanted_ref.shape[2]
    low, low_rows = partial.shape[0], partial.shape[1]
    owners, chunk = column_sum.shape[0], column_sum.shape[1]
    high = parts // low
    at_high, at_low = me // low, lax.rem(me, low)
    groups = block // LANES
    blocks = sink_ref.shape[0] // groups

    def peer(k):
        return lax.rem(me + k, parts)

    def giver(k):
        return lax.rem(me + (parts - k), parts)

    def rows_of(q):
        return pl.ds(pl.multiple_of(q * slots, slots), slots)

    def copy(stage, k, src, dst, device=None):
        return pltpu.make_async_remote_copy(
            src_ref=src,
            dst_ref=dst,
            send_sem=send_sems.at[stage, k],
            recv_sem=recv_sems.at[stage, k],
            device_id={"dom": peer(k) if device is None else device},
            device_id_type=MESH,
        )

    def each_peer(act, count=parts):
        lax.fori_loop(1, count, lambda k, c: (act(k), c)[1], 0)

    loads = [
        pltpu.make_async_copy(src, dst, load_sems.at[i])
        for i, (src, dst) in enumerate(
            (
                (w_neigh_hbm, w_neigh_ref),
                (features_hbm, features_ref),
                (mean_hbm, mean_ref),
                (w_self_hbm, w_self_ref),
            )
        )
    ]

    barrier = pltpu.get_barrier_semaphore()
    pl.semaphore_signal(barrier, inc=1, device_id={"feat": partner}, device_id_type=MESH)
    each_peer(
        lambda k: pl.semaphore_signal(
            barrier, inc=1, device_id={"dom": peer(k)}, device_id_type=MESH
        )
    )
    for load in loads:
        load.start()
    keep = (pre_ref[...] > 0).astype(F32)
    cols[half] = (grad_ref[...].astype(F32) * keep).astype(BF16)
    place = (
        lax.broadcasted_iota(jnp.int32, source_ref.shape, 0) * LANES
        + lax.broadcasted_iota(jnp.int32, source_ref.shape, 1)
    )
    live[...] = jnp.where(place < limit_ref[0], source_ref[...], -1)
    asked[me] = wanted_ref[me]
    pl.semaphore_wait(barrier, parts)

    exchange = pltpu.make_async_remote_copy(
        src_ref=cols.at[half],
        dst_ref=cols.at[half],
        send_sem=feat_sems.at[0],
        recv_sem=feat_sems.at[1],
        device_id={"feat": partner},
        device_id_type=MESH,
    )
    exchange.start()

    def request(k):
        return copy(0, k, wanted_ref.at[peer(k)], asked.at[me])

    each_peer(lambda k: request(k).start())
    def half_at(h):
        return pl.ds(pl.multiple_of(h * width, width), width)

    loads[0].wait()
    own = dot(cols[half], w_neigh_ref[:, half_at(half)], (1, 1))
    pltpu.make_async_remote_copy(
        src_ref=cols.at[half],
        dst_ref=cols.at[partner],
        send_sem=feat_sems.at[0],
        recv_sem=feat_sems.at[1],
        device_id={"feat": partner},
        device_id_type=MESH,
    ).wait_recv()

    both = jnp.concatenate([cols[0], cols[1]], axis=1)
    per_weight = low // 2
    for i, operand in enumerate((features_ref, mean_ref)):
        loads[1 + i].wait()
        part = dot(operand[...], both, (0, 0)).astype(BF16)
        for c in range(per_weight):
            partial[i * per_weight + c] = part[c * low_rows : (c + 1) * low_rows, :]

    def low_peer(k):
        return lax.rem(at_low + k, low)

    def low_giver(k):
        return lax.rem(at_low + (low - k), low)

    def high_peer(k):
        return lax.rem(at_high + k, high)

    def high_giver(k):
        return lax.rem(at_high + (high - k), high)

    def to_low(stage, k, src, dst):
        return copy(stage, k, src, dst, at_high * low + low_peer(k))

    def to_high(stage, k, src, dst):
        return copy(stage, k, src, dst, high_peer(k) * low + at_low)

    def guarded(act, owner):
        if owners == high:
            return act
        return lambda k: pl.when(owner(k) < owners)(lambda: act(k))

    def if_owner(act):
        if owners == high:
            act()
        else:
            pl.when(at_high < owners)(act)

    def scatter(k):
        return to_low(2, k, partial.at[low_peer(k)], arrived.at[at_low])

    each_peer(lambda k: scatter(k).start(), low)
    neigh = own + dot(cols[partner], w_neigh_ref[:, half_at(partner)], (1, 1))
    for g in range(masters // LANES):
        at = slice(g * LANES, (g + 1) * LANES)
        degree = columns_of(degree_ref[g : g + 1, :]).astype(F32)
        degree = jnp.concatenate([degree] * (width // LANES), axis=1)
        table[at, :] = (neigh[at, :] / degree).astype(BF16)

    each_peer(lambda k: copy(0, k, wanted_ref.at[peer(k)], asked.at[giver(k)]).wait_recv())

    batch = 8 if parts % 8 == 0 else 1
    hub = lax.broadcasted_iota(jnp.int32, (HUBS, slots), 0)

    def batch_at(i):
        return pl.ds(pl.multiple_of(i * batch * slots, batch * slots), batch * slots)

    def answer(i, c):
        hit = jnp.concatenate(
            [
                jnp.where(hub == asked[i * batch + j], jnp.ones((), BF16), jnp.zeros((), BF16))
                for j in range(batch)
            ],
            axis=1,
        )
        hits[i] = hit
        replies[batch_at(i), :] = dot(hit, table[:HUBS, :], (0, 0)).astype(BF16)
        return c

    lax.fori_loop(0, parts // batch, answer, 0)
    mirrors[rows_of(me), :] = replies[rows_of(me), :]

    def reply(k):
        return copy(1, k, replies.at[rows_of(peer(k)), :], mirrors.at[rows_of(me), :])

    each_peer(lambda k: reply(k).start())

    def block_at(b):
        return pl.ds(pl.multiple_of(b * groups, groups), groups)

    def edges_at(b):
        return pl.ds(pl.multiple_of(b * block, block), block)

    def from_masters(b, c):
        pick = pick_rows(sink_ref[block_at(b), :], 0, masters)
        picked[edges_at(b), :] = dot(pick, table[...], (1, 0)).astype(BF16)
        return c

    lax.fori_loop(0, blocks, from_masters, 0)

    each_peer(
        lambda k: to_low(2, k, partial.at[low_peer(k)], arrived.at[low_giver(k)]).wait_recv(), low
    )
    total = lax.fori_loop(
        1,
        low,
        lambda k, t: t + arrived[low_giver(k)].astype(F32),
        partial[at_low].astype(F32),
    ).astype(BF16)
    for c in range(owners):
        column_sum[c] = total[c * chunk : (c + 1) * chunk, :]

    def column_place():
        return lax.rem(at_high, owners)

    def scatter_high(k):
        return to_high(
            4, k, column_sum.at[lax.rem(high_peer(k), owners)], column_arrived.at[at_high]
        )

    each_peer(guarded(lambda k: scatter_high(k).start(), high_peer), high)

    each_peer(
        lambda k: copy(
            1, k, replies.at[rows_of(peer(k)), :], mirrors.at[rows_of(giver(k)), :]
        ).wait_recv()
    )
    mirror_sum[...] = jnp.zeros_like(mirror_sum)
    mirror_count = mirrors.shape[0]

    def from_mirrors(b, c):
        pick = pick_rows(sink_ref[block_at(b), :], masters, mirror_count)
        more = dot(pick, mirrors[...], (1, 0)).astype(BF16)
        row = picked[edges_at(b), :] + more
        picked[edges_at(b), :] = row
        return c

    lax.fori_loop(0, blocks, from_mirrors, 0)

    def column_spread(k):
        return to_high(5, k, column_total.at[column_place()], column_total.at[column_place()])

    def reduce_column():
        each_peer(
            lambda k: to_high(
                4,
                k,
                column_sum.at[lax.rem(high_peer(k), owners)],
                column_arrived.at[high_giver(k)],
            ).wait_recv(),
            high,
        )
        column_total[column_place()] = lax.fori_loop(
            1,
            high,
            lambda k, t: t + column_arrived[high_giver(k)].astype(F32),
            column_sum[column_place()].astype(F32),
        ).astype(BF16)
        each_peer(lambda k: column_spread(k).start(), high)

    if_owner(reduce_column)

    def to_mirrors(b, c):
        put = put_rows(live[block_at(b), :], masters, mirror_count)
        mirror_sum[...] += dot(put, picked[edges_at(b), :], (1, 0))
        return c

    lax.fori_loop(0, blocks, to_mirrors, 0)
    returns[...] = mirror_sum[...].astype(BF16)
    returned[rows_of(me), :] = returns[rows_of(me), :]

    def give_back(k):
        return copy(3, k, returns.at[rows_of(peer(k)), :], returned.at[rows_of(me), :])

    each_peer(lambda k: give_back(k).start())

    each_peer(
        guarded(
            lambda k: to_high(
                5,
                k,
                column_total.at[column_place()],
                column_total.at[lax.rem(high_giver(k), owners)],
            ).wait_recv(),
            high_giver,
        ),
        high,
    )
    full[at_low] = column_total[...]

    def spread(k):
        return to_low(6, k, column_total, full.at[at_low])

    each_peer(lambda k: spread(k).start(), low)

    loads[3].wait()
    master_sum[...] = dot(cols[0], w_self_ref[:, :width], (1, 1)) + dot(
        cols[1], w_self_ref[:, width:], (1, 1)
    )

    def to_masters(b, c):
        put = put_rows(live[block_at(b), :], 0, masters)
        master_sum[...] += dot(put, picked[edges_at(b), :], (1, 0))
        return c

    lax.fori_loop(0, blocks, to_masters, 0)

    each_peer(
        lambda k: copy(
            3, k, returns.at[rows_of(peer(k)), :], returned.at[rows_of(giver(k)), :]
        ).wait_recv()
    )
    hub_sum = lax.fori_loop(
        0,
        parts // batch,
        lambda i, t: t + dot(hits[i], returned[batch_at(i), :], (1, 0)),
        master_sum[:HUBS, :],
    )
    out_ref[:HUBS, :] = hub_sum.astype(BF16)
    out_ref[HUBS:, :] = master_sum[HUBS:, :].astype(BF16)

    each_peer(lambda k: to_low(6, k, column_total, full.at[low_giver(k)]).wait_recv(), low)
    weights_ref[...] = full[...]

    exchange.wait_send()
    each_peer(lambda k: request(k).wait_send())
    each_peer(lambda k: reply(k).wait_send())
    each_peer(lambda k: give_back(k).wait_send())
    each_peer(lambda k: scatter(k).wait_send(), low)
    each_peer(guarded(lambda k: scatter_high(k).wait_send(), high_peer), high)
    if_owner(lambda: each_peer(lambda k: column_spread(k).wait_send(), high))
    each_peer(lambda k: spread(k).wait_send(), low)


def on_device(
    features,
    grad_out,
    pre_act,
    neigh_mean,
    w_self,
    w_neigh,
    edge_from,
    edge_to,
    edge_count,
    mirror_master,
    degrees,
):
    masters, width = features.shape
    parts = lax.axis_size("dom")
    mirror_count = mirror_master.shape[0]
    slots = mirror_count // parts
    edges = edge_from.shape[0]
    full = w_self.shape[1]
    weight_rows = 2 * w_self.shape[0]
    low = 2
    while parts % (4 * low) == 0 and 4 * low * low <= parts:
        low *= 2
    low_rows = weight_rows // low
    owners = min(parts // low, low_rows // 16)
    chunk = low_rows // owners
    batch = 8 if parts % 8 == 0 else 1
    block = min(edges, 2048 if masters + mirror_count <= 2048 else 256)
    vmem = pl.BlockSpec(memory_space=pltpu.VMEM)
    anywhere = pl.BlockSpec(memory_space=pl.ANY)
    input_grad, weights = pl.pallas_call(
        functools.partial(layer_kernel, parts, block),
        out_shape=(
            jax.ShapeDtypeStruct((masters, width), BF16),
            jax.ShapeDtypeStruct((low, owners, chunk, full), BF16),
        ),
        in_specs=[pl.BlockSpec(memory_space=pltpu.SMEM)] + [vmem] * 2 + [anywhere] * 4 + [vmem] * 4,
        out_specs=(vmem, vmem),
        scratch_shapes=[
            pltpu.VMEM(features.shape, BF16),
            pltpu.VMEM(features.shape, BF16),
            pltpu.VMEM(w_self.shape, BF16),
            pltpu.VMEM(w_self.shape, BF16),
            pltpu.VMEM((2, masters, width), BF16),
            pltpu.VMEM((edges // LANES, LANES), jnp.int32),
            pltpu.VMEM((masters, width), BF16),
            pltpu.VMEM((parts, 1, slots), jnp.int32),
            pltpu.VMEM((mirror_count, width), BF16),
            pltpu.VMEM((mirror_count, width), BF16),
            pltpu.VMEM((edges, width), BF16),
            pltpu.VMEM((masters, width), F32),
            pltpu.VMEM((mirror_count, width), F32),
            pltpu.VMEM((mirror_count, width), BF16),
            pltpu.VMEM((mirror_count, width), BF16),
            pltpu.VMEM((parts // batch, HUBS, batch * slots), BF16),
            pltpu.VMEM((low, low_rows, full), BF16),
            pltpu.VMEM((low, low_rows, full), BF16),
            pltpu.VMEM((owners, chunk, full), BF16),
            pltpu.VMEM((parts // low, chunk, full), BF16),
            pltpu.VMEM((owners, chunk, full), BF16),
            pltpu.VMEM((low, owners, chunk, full), BF16),
            pltpu.SemaphoreType.DMA((4,)),
            pltpu.SemaphoreType.DMA((2,)),
            pltpu.SemaphoreType.DMA((7, parts)),
            pltpu.SemaphoreType.DMA((7, parts)),
        ],
        compiler_params=pltpu.CompilerParams(
            collective_id=0, has_side_effects=True, vmem_limit_bytes=60 * 2**20
        ),
    )(
        edge_count,
        grad_out,
        pre_act,
        features,
        neigh_mean,
        w_self,
        w_neigh,
        edge_from.reshape(-1, LANES),
        edge_to.reshape(-1, LANES),
        mirror_master.reshape(parts, 1, slots),
        degrees.reshape(-1, LANES),
    )
    weights = weights.reshape(2, w_self.shape[0], full).astype(F32)
    return (input_grad, weights[0], weights[1])


def solution(mesh):
    placed = (
        P("dom", "feat"),
        P("dom", "feat"),
        P("dom", "feat"),
        P("dom", "feat"),
        P("feat", None),
        P("feat", None),
        P("dom"),
        P("dom"),
        P("dom"),
        P("dom"),
        P("dom"),
    )
    return jax.shard_map(
        on_device,
        mesh=mesh,
        in_specs=placed,
        out_specs=(P("dom", "feat"), P("feat", None), P("feat", None)),
        check_vma=False,
    )
```
